32 devices in a mesh: dp: 4 (over y, x), mp: 8 (over z, core).
Axes of the slice: x: 2, y: 2, z: 4, core: 2. Of those that a mesh axis runs over, the one named last changes fastest.
Arguments:
- residual_in: bfloat16 [512, 3584], P('dp', 'mp'), may hold values from -6 to 6
- pre_gain: float32 [3584], replicated, may hold values from 0.5 to 1.5
- post_gain: float32 [3584], replicated, may hold values from 0.5 to 1.5
- w_gate: bfloat16 [3584, 14336], P(None, 'mp'), may hold values from -0.09375 to 0.09375
- w_up: bfloat16 [3584, 14336], P(None, 'mp'), may hold values from -0.09375 to 0.09375
- w_down: bfloat16 [14336, 3584], P('mp'), may hold values from -0.046875 to 0.046875
- w_enc: bfloat16 [3584, 16384], P(None, ('dp', 'mp')), may hold values from -0.09375 to 0.09375
- b_enc: float32 [16384], P(('dp', 'mp')), may hold values from -2.5 to 2.5
- threshold: float32 [16384], P(('dp', 'mp')), may hold values from 0.1 to 1
- w_dec: bfloat16 [16384, 3584], P(('dp', 'mp')), may hold values from -0.046875 to 0.046875
- b_dec: float32 [3584], replicated, may hold values from -1.5 to 1.5
Outputs:
- loss_value: float32 [], replicated
- d_w_enc: bfloat16 [3584, 16384], P(None, ('dp', 'mp'))
- d_w_dec: bfloat16 [16384, 3584], P(('dp', 'mp'))
- d_b_enc: float32 [16384], P(('dp', 'mp'))
- d_threshold: float32 [16384], P(('dp', 'mp'))
- d_b_dec: float32 [3584], replicated
The draws below stay inside these ranges and needn't reach their ends.
All inputs are finite; a program needn't handle non-finite values.
Results may differ from the reference program's by a relative error of at most 0.014.
The reference program's roundings to bfloat16 on the way count: a program that leaves them out, or rounds other values in their place, can miss the bound.
Values may be sent and summed in bfloat16 or wider, within the bound.
No kernel may reach another device: no remote copies, remote signals or barrier semaphores. Data moves between devices by JAX's collectives and lax.ppermute only.
A program may use at most 128 MiB of HBM per device.

```python
import math
import jax
import jax.numpy as jnp
from jax import lax

D = 3584
FF = 14336
TOKENS = 512
FEATURES = 16384


def draw_b_enc(key, part):
    position = (jnp.arange(FEATURES).astype(jnp.float32) + 0.5) / FEATURES
    noise = 0.3 * jax.random.normal(jax.random.fold_in(key, 11), (FEATURES,), jnp.float32)
    values = -2.0 + 4.0 * position + noise
    return jnp.clip(values, -2.5, 2.5).astype(jnp.float32)


def steps_of(own_key, extent, pieces, low, top_value):
    def one(axis_at, blocks):
        draws = jax.random.uniform(jax.random.fold_in(jax.random.fold_in(own_key, 6), axis_at), (blocks,), jnp.float32, low / len(pieces), top_value / len(pieces))
        return jnp.repeat(jnp.exp(draws), extent[axis_at] // blocks).reshape((-1,) + (1,) * (len(extent) - axis_at - 1))

    level = one(*pieces[0])
    for cut in pieces[1:]:
        level = level * one(*cut)
    return level


def gaussian(own_key, dims, deviation, most, pieces=(), held_as=jnp.bfloat16):
    level = steps_of(own_key, dims, pieces, -0.22, 0.18) if pieces else 1.0
    entries = jax.random.normal(own_key, dims, jnp.float32) * deviation * level
    return jnp.minimum(jnp.maximum(entries, -most), most).astype(held_as)


def setup_inputs(seed: int = 0) -> dict:
    splits = jax.random.split(jax.random.key(seed), 12)
    residual_in = gaussian(splits[0], (TOKENS, D), 1.0, 6.0, ((0, 4), (1, 8)))
    pre_gain = jnp.clip(1.0 + 0.1 * jax.random.normal(splits[1], (D,), jnp.float32), 0.5, 1.5)
    post_gain = jnp.clip(1.0 + 0.1 * jax.random.normal(splits[2], (D,), jnp.float32), 0.5, 1.5)
    w_gate = gaussian(splits[3], (D, FF), D ** -0.5, 0.09375, ((1, 8),))
    w_up = gaussian(splits[4], (D, FF), D ** -0.5, 0.09375, ((1, 8),))
    w_down = gaussian(splits[5], (FF, D), FF ** -0.5, 0.046875, ((0, 8),))
    w_enc = gaussian(splits[6], (D, FEATURES), D ** -0.5, 0.09375, ((1, 32),))
    b_enc = draw_b_enc(jax.random.fold_in(splits[11], 71), 0)
    threshold = jnp.clip(jnp.exp(math.log(1.0) - 2.3025851 * jax.random.uniform(splits[8], (FEATURES,), jnp.float32) ** steps_of(splits[8], (FEATURES,), ((0, 32),), -0.2, 0.2)), 0.1, 1.0)
    w_dec = gaussian(splits[9], (FEATURES, D), FEATURES ** -0.5, 0.046875, ((0, 32),))
    b_dec = gaussian(splits[10], (D,), 0.3, 1.5, (), jnp.float32)
    return dict(residual_in=residual_in, pre_gain=pre_gain, post_gain=post_gain, w_gate=w_gate, w_up=w_up, w_down=w_down, w_enc=w_enc, b_enc=b_enc, threshold=threshold, w_dec=w_dec, b_dec=b_dec)


norm_eps = 1e-06
gate_band = 0.1
sparsity_coef = 0.05

def rms_norm(values, gain):
    return values * lax.rsqrt(lax.optimization_barrier(jnp.mean(values * values, axis=-1, keepdims=True)) + norm_eps) * gain

def reference(residual_in, pre_gain, post_gain, w_gate, w_up, w_down, w_enc, b_enc, threshold, w_dec, b_dec):
    resid_wide = residual_in.astype(jnp.float32)
    normed = rms_norm(resid_wide, pre_gain).astype(jnp.bfloat16)
    gate_out = jnp.dot(normed, w_gate, preferred_element_type=jnp.float32)
    up_out = jnp.dot(normed, w_up, preferred_element_type=jnp.float32)
    hidden = (jax.nn.gelu(gate_out, approximate=True) * up_out).astype(jnp.bfloat16)
    block_out = jnp.dot(hidden, w_down, preferred_element_type=jnp.float32)
    layer_out = (resid_wide + rms_norm(block_out, post_gain)).astype(jnp.bfloat16)
    pre_act = jnp.dot(layer_out, w_enc, preferred_element_type=jnp.float32) + b_enc
    soft = jax.nn.sigmoid((pre_act - threshold) / gate_band)
    feat_bf = (pre_act * soft).astype(jnp.bfloat16)
    error_t = jnp.dot(feat_bf, w_dec, preferred_element_type=jnp.float32) + b_dec - layer_out.astype(jnp.float32)
    loss_value = (0.5 * jnp.sum(error_t * error_t) + sparsity_coef * jnp.sum(soft)) / (TOKENS * D)
    d_b_dec = lax.optimization_barrier(jnp.sum(error_t, axis=0))
    err_bf = error_t.astype(jnp.bfloat16)
    d_w_dec = jnp.dot(feat_bf.T, err_bf, preferred_element_type=jnp.float32).astype(jnp.bfloat16)
    grad_feat = jnp.dot(err_bf, w_dec.T, preferred_element_type=jnp.float32)
    slope = soft * (1.0 - soft) / gate_band
    side_term = (grad_feat * pre_act + sparsity_coef) * slope
    grad_pre = grad_feat * soft + side_term
    d_threshold = -lax.optimization_barrier(jnp.sum(side_term, axis=0))
    d_b_enc = lax.optimization_barrier(jnp.sum(grad_pre, axis=0))
    d_w_enc = jnp.dot(layer_out.T, grad_pre.astype(jnp.bfloat16), preferred_element_type=jnp.float32).astype(jnp.bfloat16)
    return (loss_value, d_w_enc, d_w_dec, d_b_enc, d_threshold, d_b_dec)
```

```python
import jax
import jax.numpy as jnp
from jax import lax
from jax.sharding import PartitionSpec as P

norm_eps = 1e-06
gate_band = 0.1
sparsity_coef = 0.05


f32 = jnp.float32
bf16 = jnp.bfloat16
both = ("dp", "mp")


def dot(left, right, left_dim, right_dim):
    return lax.dot_general(
        left, right, (((left_dim,), (right_dim,)), ((), ())), preferred_element_type=f32
    )


def program(n_dp, n_mp):
    n_z = n_mp // 2
    everyone = [(d, m) for d in range(n_dp) for m in range(n_mp)]

    def swap(value, dp_bits=0, z_bits=0, core_bit=0):
        pairs = [
            (d * n_mp + m, (d ^ dp_bits) * n_mp + (m ^ (2 * z_bits + core_bit)))
            for d, m in everyone
        ]
        return lax.ppermute(value, both, pairs)

    def gather_column(block):
        return [block] + [swap(block, z_bits=dz) for dz in range(1, n_z)]

    def gather_all(block):
        rows = jnp.concatenate(gather_column(block), axis=0)
        half = rows.shape[0] // 2
        planes = [rows] + [swap(rows, dp_bits=b) for b in range(1, min(n_dp, 3))]
        if n_dp == 4:
            planes.append(
                jnp.concatenate(
                    [
                        swap(planes[2][:half], dp_bits=1),
                        swap(planes[1][half:], dp_bits=2),
                    ],
                    axis=0,
                )
            )
        else:
            planes += [swap(rows, dp_bits=b) for b in range(3, n_dp)]
        others = [swap(plane, core_bit=1) for plane in planes]
        return jnp.concatenate(planes + others, axis=0)

    def scatter_column(total):
        count = total.shape[0] // n_z
        out = total[:count]
        for dz in range(1, n_z):
            out = out + swap(
                total[dz * count : (dz + 1) * count].astype(bf16), z_bits=dz
            ).astype(f32)
        return out

    def scatter_all(part):
        cut = part.shape[0] // 2
        mine = part[:cut] + swap(part[cut:].astype(bf16), core_bit=1).astype(f32)
        count = cut // n_dp
        planes = [mine[i * count : (i + 1) * count] for i in range(n_dp)]
        if n_dp == 4:
            half = count // 2
            far = planes[3].astype(bf16)
            via_x = swap(far[:half], dp_bits=1).astype(f32)
            via_y = swap(far[half:], dp_bits=2).astype(f32)
            to_y = jnp.concatenate([planes[2][:half] + via_x, planes[2][half:]], axis=0)
            to_x = jnp.concatenate([planes[1][:half], planes[1][half:] + via_y], axis=0)
            own = (
                planes[0]
                + swap(to_x.astype(bf16), dp_bits=1).astype(f32)
                + swap(to_y.astype(bf16), dp_bits=2).astype(f32)
            )
        else:
            own = planes[0]
            for b in range(1, n_dp):
                own = own + swap(planes[b].astype(bf16), dp_bits=b).astype(f32)
        return scatter_column(own)

    def sum_everywhere(value):
        for bit in range((n_dp - 1).bit_length()):
            value = value + swap(value, dp_bits=1 << bit)
        for bit in range((n_z - 1).bit_length()):
            value = value + swap(value, z_bits=1 << bit)
        return value + swap(value, core_bit=1)

    def local(
        residual_in, pre_gain, post_gain, w_gate, w_up, w_down, w_enc, b_enc, threshold, w_dec, b_dec
    ):
        tokens, width = residual_in.shape[0] * n_dp, w_gate.shape[0]
        at_mp = lax.axis_index("mp")
        at_z, at_core = at_mp // 2, at_mp % 2

        full_rows = lax.all_gather(residual_in, "mp", axis=1, tiled=True)
        resid_wide = full_rows.astype(f32)
        normed = (
            resid_wide
            * lax.rsqrt(jnp.mean(resid_wide * resid_wide, axis=1, keepdims=True) + norm_eps)
            * pre_gain[None, :]
        ).astype(bf16)
        gate_out = dot(normed, w_gate, 1, 0)
        up_out = dot(normed, w_up, 1, 0)
        hidden = (jax.nn.gelu(gate_out, approximate=True) * up_out).astype(bf16)
        out_part = dot(hidden, w_down, 1, 0)

        count = out_part.shape[0] // n_mp
        split = out_part.reshape(n_z, 2, count, width)
        keep = lax.dynamic_index_in_dim(split, at_core, 1, keepdims=False)
        give = lax.dynamic_index_in_dim(split, 1 - at_core, 1, keepdims=False)
        pair = keep + swap(give.astype(bf16), core_bit=1).astype(f32)
        block = lax.dynamic_index_in_dim(pair, at_z, 0, keepdims=False)
        for dz in range(1, n_z):
            piece = lax.dynamic_index_in_dim(pair, at_z ^ dz, 0, keepdims=False)
            block = block + swap(piece.astype(bf16), z_bits=dz).astype(f32)
        own_rows = lax.dynamic_slice_in_dim(full_rows, at_mp * count, count, 0).astype(f32)
        layer_own = (
            own_rows
            + block
            * lax.rsqrt(jnp.mean(block * block, axis=1, keepdims=True) + norm_eps)
            * post_gain[None, :]
        ).astype(bf16)

        layer_out = gather_all(layer_own)
        pre_act = dot(layer_out, w_enc, 1, 0) + b_enc[None, :]
        soft = jax.nn.sigmoid((pre_act - threshold[None, :]) / gate_band)
        feat_bf = (pre_act * soft).astype(bf16)
        gate_part = jnp.sum(soft)
        recon_own = scatter_all(dot(feat_bf, w_dec, 1, 0))
        error_own = recon_own + b_dec[None, :] - layer_own.astype(f32)
        err_all = gather_all(error_own.astype(bf16))

        loss_part = 0.5 * jnp.sum(error_own * error_own) + sparsity_coef * gate_part
        lanes = 128
        tail = jnp.zeros((lanes,), f32).at[0].set(loss_part)
        sums = jnp.concatenate([jnp.sum(error_own, axis=0), tail]).reshape(-1, lanes)
        sums = sum_everywhere(sums).reshape(-1)
        grad_bdec = sums[:width]
        loss_value = sums[width] / (tokens * width)

        grad_wdec = dot(feat_bf, err_all, 0, 0).astype(bf16)
        grad_feat = dot(err_all, w_dec, 1, 1)
        slope = soft * (1.0 - soft) / gate_band
        side_term = (grad_feat * pre_act + sparsity_coef) * slope
        grad_pre = grad_feat * soft + side_term
        grad_thresh = -jnp.sum(side_term, axis=0)
        grad_benc = jnp.sum(grad_pre, axis=0)
        grad_wenc = dot(layer_out, grad_pre.astype(bf16), 0, 0).astype(bf16)
        return (loss_value, grad_wenc, grad_wdec, grad_benc, grad_thresh, grad_bdec)

    return local


def solution(mesh):
    placed = (
        P("dp", "mp"),
        P(),
        P(),
        P(None, "mp"),
        P(None, "mp"),
        P("mp", None),
        P(None, both),
        P(both),
        P(both),
        P(both, None),
        P(),
    )
    return jax.shard_map(
        program(mesh.shape["dp"], mesh.shape["mp"]),
        mesh=mesh,
        in_specs=placed,
        out_specs=(P(), P(None, both), P(both, None), P(both), P(both), P()),
        check_vma=False,
    )
```

```python
import functools

import jax
import jax.numpy as jnp
from jax import lax
from jax.experimental import pallas as pl
from jax.experimental.pallas import tpu as pltpu
from jax.sharding import PartitionSpec as P


norm_eps = 1e-06
gate_band = 0.1
sparsity_coef = 0.05


f32 = jnp.float32
bf16 = jnp.bfloat16
both = ("dp", "mp")


def dot(left, right, left_dim, right_dim):
    return lax.dot_general(
        left, right, (((left_dim,), (right_dim,)), ((), ())), preferred_element_type=f32
    )


def finish(n_parts, entries, thr_ref, w_dec_ref, *rest):
    pairs = [rest[2 * i : 2 * i + 2] for i in range(3 + 2 * n_parts)]
    pre_refs, partial_refs, feat_refs = pairs[:3]
    layer_refs, err_refs = pairs[3 : 3 + n_parts], pairs[3 + n_parts :]
    wenc_ref, wdec_ref, gthr_ref, gbenc_ref, gbdec_ref, loss_ref, buffer, sems = rest[-8:]
    span = err_refs[0][0].shape[1]
    n_slots = buffer.shape[0]
    step = buffer.shape[1]
    copies = []

    def send(value, target):
        index = len(copies)
        slot = index % n_slots
        if index >= n_slots:
            copies[index - n_slots].wait()
        rows, cols = value.shape
        block = buffer.at[slot, pl.ds(0, rows), pl.ds(0, cols)]
        block[...] = value.astype(bf16)
        copy = pltpu.make_async_copy(block, target, sems.at[slot])
        copy.start()
        copies.append(copy)

    def grad_wdec(i):
        for low in range(0, span, step):
            size = min(step, span - low)
            value = sum(
                dot(feat[...], err[:, low : low + size], 0, 0)
                for feat, err in zip(feat_refs, err_refs[i])
            )
            send(value, wdec_ref.at[:, pl.ds(i * span + low, size)])
            ones = jnp.ones((8, err_refs[i][0].shape[0]), bf16)
            gbdec_ref[:, i * span + low : i * span + low + size] = sum(
                dot(ones, err[:, low : low + size], 1, 0)[:1] for err in err_refs[i]
            )

    for i in range(n_parts - 1):
        grad_wdec(i)

    weight = w_dec_ref[:, (n_parts - 1) * span :]
    grads, sums_thr, sums_benc = [], 0.0, 0.0
    for pre_ref, partial_ref, err_ref in zip(pre_refs, partial_refs, err_refs[-1]):
        grad_feat = partial_ref[...] + dot(err_ref[:, :span], weight, 1, 1)
        pre = pre_ref[...]
        soft = jax.nn.sigmoid((pre - thr_ref[...]) / gate_band)
        slope = soft * (1.0 - soft) / gate_band
        side_term = (grad_feat * pre + sparsity_coef) * slope
        grad = grad_feat * soft + side_term
        sums_thr = sums_thr - jnp.sum(side_term, axis=0, keepdims=True)
        sums_benc = sums_benc + jnp.sum(grad, axis=0, keepdims=True)
        grads.append(grad.astype(bf16))
    shares = sum(
        jnp.sum(err_ref[:, span:].astype(f32), axis=0, keepdims=True)
        for err_ref in err_refs[-1]
    )
    loss_ref[0, 0] = jnp.sum(shares) / entries
    gthr_ref[...] = sums_thr
    gbenc_ref[...] = sums_benc
    for i, layers in enumerate(layer_refs):
        for low in range(0, span, step):
            size = min(step, span - low)
            value = sum(
                dot(layer[:, low : low + size], grad, 0, 0)
                for layer, grad in zip(layers, grads)
            )
            send(value, wenc_ref.at[pl.ds(i * span + low, size), :])
    grad_wdec(n_parts - 1)
    for copy in copies[-n_slots:]:
        copy.wait()


def program(n_dp, n_mp):
    n_z = n_mp // 2
    everyone = [(d, m) for d in range(n_dp) for m in range(n_mp)]

    bits_of = lambda count: [1 << i for i in range((count - 1).bit_length())]
    z_steps = [(0, bit) for bit in bits_of(n_z)]
    dp_steps = [(bit, 0) for bit in bits_of(n_dp)]
    orders = (z_steps + dp_steps, z_steps[::-1] + dp_steps[::-1])
    steps = len(orders[0])

    def other_core(value):
        return lax.ppermute(
            value, both, [(d * n_mp + m, d * n_mp + (m ^ 1)) for d, m in everyone]
        )

    def exchange(value, step):
        pairs = []
        for d, m in everyone:
            dp_bits, z_bits = orders[m % 2][step]
            pairs.append((d * n_mp + m, (d ^ dp_bits) * n_mp + (m ^ (2 * z_bits))))
        return lax.ppermute(value, both, pairs)

    def gather(rows):
        for step in range(steps):
            got = exchange(rows, step)
            rows = jnp.concatenate([rows, got], axis=0)
        return rows

    def scatter(total, count):
        for step in reversed(range(count)):
            cut = total.shape[0] // 2
            give = total[cut:].astype(bf16)
            got = exchange(give, step)
            total = total[:cut] + got.astype(f32)
        return total

    def whole_step(
        residual_in, pre_gain, post_gain, w_gate, w_up, w_down, w_enc, b_enc, threshold, w_dec, b_dec
    ):
        tokens, width = residual_in.shape[0] * n_dp, w_gate.shape[0]
        at_mp = lax.axis_index("mp")
        at_z, at_core = at_mp // 2, at_mp % 2
        count = residual_in.shape[0] // n_mp

        def columns(cuts):
            span = width // cuts
            return [slice(i * span, (i + 1) * span) for i in range(cuts)]

        full_rows = lax.all_gather(residual_in, "mp", axis=1, tiled=True)
        slot = jnp.arange(n_z)
        turned = sum(
            ((slot >> i) & 1) << (len(z_steps) - 1 - i) for i in range(len(z_steps))
        )
        straight = jnp.where(at_core == 0, slot, turned)
        crossed = jnp.where(at_core == 0, turned, slot)
        owner = jnp.concatenate(
            [2 * (at_z ^ straight) + at_core, 2 * (at_z ^ crossed) + 1 - at_core]
        )
        source = (owner[:, None] * count + jnp.arange(count)[None, :]).reshape(-1)
        pick = (source[:, None] == jnp.arange(source.shape[0])[None, :]).astype(bf16)
        full_rows = dot(pick, full_rows, 1, 0).astype(bf16)

        resid_wide = full_rows.astype(f32)
        normed = (
            resid_wide
            * lax.rsqrt(jnp.mean(resid_wide * resid_wide, axis=1, keepdims=True) + norm_eps)
            * pre_gain[None, :]
        ).astype(bf16)
        gate_out = dot(normed, w_gate, 1, 0)
        up_out = dot(normed, w_up, 1, 0)
        hidden = (jax.nn.gelu(gate_out, approximate=True) * up_out).astype(bf16)
        hidden = lax.optimization_barrier(hidden)
        half = hidden.shape[0] // 2
        blocks = []
        for cols in columns(2):
            part = dot(hidden, w_down[:, cols], 1, 0)
            mine = part[:half] + other_core(part[half:].astype(bf16)).astype(f32)
            blocks.append(scatter(mine, len(z_steps)))
        block = jnp.concatenate(blocks, axis=1)
        layer_own = (
            resid_wide[:count]
            + block
            * lax.rsqrt(jnp.mean(block * block, axis=1, keepdims=True) + norm_eps)
            * post_gain[None, :]
        ).astype(bf16)

        layer_out = []
        for cols in columns(2):
            near = gather(layer_own[:, cols])
            layer_out.append((near, other_core(near)))
        sides = range(2)

        def over(parts, weight, dim, side, leave=0):
            return sum(
                dot(part[side], weight(cols), 1, dim)
                for part, cols in list(zip(parts, columns(len(parts))))[: len(parts) - leave]
            )

        pre_act = [
            over(layer_out, lambda cols: w_enc[cols, :], 0, side) + b_enc[None, :]
            for side in sides
        ]
        soft = [jax.nn.sigmoid((pre - threshold[None, :]) / gate_band) for pre in pre_act]
        feat = [(pre * open_).astype(bf16) for pre, open_ in zip(pre_act, soft)]
        lanes = 128

        def fold(row):
            return sum(row[:, i : i + lanes] for i in range(0, row.shape[1], lanes))

        open_total = sum(
            fold(jnp.sum(open_, axis=0, keepdims=True)) for open_ in soft
        )
        error_own = []
        for cols in columns(2):
            far = other_core(dot(feat[1], w_dec[:, cols], 1, 0).astype(bf16))
            mine = dot(feat[0], w_dec[:, cols], 1, 0) + far.astype(f32)
            recon = scatter(mine, steps)
            error_own.append(recon + b_dec[None, cols] - layer_own[:, cols].astype(f32))

        rest = 0.5 * sum(
            fold(jnp.sum(error * error, axis=0, keepdims=True)) for error in error_own
        ) + sparsity_coef * open_total
        row = jnp.arange(count)[:, None]
        extra = jnp.zeros((count, lanes), f32)
        for i in range(3):
            term = lax.reduce_precision(rest, 8, 7)
            extra = jnp.where(row == i, term, extra)
            rest = rest - term
        extra = extra.astype(bf16)

        err_all = []
        for i, error in enumerate(error_own):
            rows = error.astype(bf16)
            if i == len(error_own) - 1:
                rows = jnp.concatenate([rows, extra], axis=1)
            near = gather(rows)
            err_all.append((near, other_core(near)))

        vmem = pl.BlockSpec(memory_space=pltpu.VMEM)
        hbm = pl.BlockSpec(memory_space=pl.ANY)
        features = w_enc.shape[1]
        pairs = [pre_act]
        pairs.append(
            [over(err_all, lambda cols: w_dec[:, cols], 1, side, 1) for side in sides]
        )
        pairs += [feat] + layer_out + err_all
        operands = [threshold[None, :], w_dec] + [part for pair in pairs for part in pair]
        n_slots = 4
        grad_wenc, grad_wdec, grad_thresh, grad_benc, grad_bdec, shares = pl.pallas_call(
            functools.partial(finish, len(err_all), float(tokens * width)),
            out_shape=(
                jax.ShapeDtypeStruct((width, features), bf16),
                jax.ShapeDtypeStruct((features, width), bf16),
                jax.ShapeDtypeStruct((1, features), f32),
                jax.ShapeDtypeStruct((1, features), f32),
                jax.ShapeDtypeStruct((1, width), f32),
                jax.ShapeDtypeStruct((1, 1), f32),
            ),
            in_specs=[vmem] * len(operands),
            out_specs=(hbm, hbm, vmem, vmem, vmem, pl.BlockSpec(memory_space=pltpu.SMEM)),
            scratch_shapes=[
                pltpu.VMEM((n_slots, 512, 512), bf16),
                pltpu.SemaphoreType.DMA((n_slots,)),
            ],
            compiler_params=pltpu.CompilerParams(vmem_limit_bytes=40 * 2**20),
            name="finish",
        )(*operands)
        grad_thresh, grad_benc, grad_bdec = grad_thresh[0], grad_benc[0], grad_bdec[0]
        loss_value = shares[0, 0]
        return (loss_value, grad_wenc, grad_wdec, grad_benc, grad_thresh, grad_bdec)

    return whole_step


def solution(mesh):
    placed = (
        P("dp", "mp"),
        P(),
        P(),
        P(None, "mp"),
        P(None, "mp"),
        P("mp", None),
        P(None, both),
        P(both),
        P(both),
        P(both, None),
        P(),
    )
    return jax.shard_map(
        program(mesh.shape["dp"], mesh.shape["mp"]),
        mesh=mesh,
        in_specs=placed,
        out_specs=(P(), P(None, both), P(both, None), P(both), P(both), P()),
        check_vma=False,
    )
```

```python
import functools

import jax
import jax.numpy as jnp
from jax import lax
from jax.experimental import pallas as pl
from jax.experimental.pallas import tpu as pltpu
from jax.sharding import PartitionSpec as P


norm_eps = 1e-06
gate_band = 0.1
sparsity_coef = 0.05


f32 = jnp.float32
bf16 = jnp.bfloat16
both = ("dp", "mp")


def dot(left, right, left_dim, right_dim):
    return lax.dot_general(
        left, right, (((left_dim,), (right_dim,)), ((), ())), preferred_element_type=f32
    )


def turn_body(near_ref, far_ref, turned_ref):
    count = near_ref.shape[0]
    turned_ref[:, :count] = near_ref[...].T
    turned_ref[:, count:] = far_ref[...].T


def row_body(source_ref, row_ref):
    row_ref[...] = source_ref[...]


def row_of(values):
    vmem = pl.BlockSpec(memory_space=pltpu.VMEM)
    return pl.pallas_call(
        row_body,
        out_shape=jax.ShapeDtypeStruct((1, values.shape[0]), values.dtype),
        in_specs=[vmem],
        out_specs=vmem,
        name="row",
    )(values[None, :])


def side_by_side(pair):
    near, far = pair
    vmem = pl.BlockSpec(memory_space=pltpu.VMEM)
    return pl.pallas_call(
        turn_body,
        out_shape=jax.ShapeDtypeStruct((near.shape[1], 2 * near.shape[0]), near.dtype),
        in_specs=[vmem] * 2,
        out_specs=vmem,
        compiler_params=pltpu.CompilerParams(vmem_limit_bytes=40 * 2**20),
        name="turn",
    )(near, far)


def sender(buffer, sems):
    n_slots = buffer.shape[0]
    copies = []

    def send(value, target):
        index = len(copies)
        slot = index % n_slots
        if index >= n_slots:
            copies[index - n_slots].wait()
        rows, cols = value.shape
        block = buffer.at[slot, pl.ds(0, rows), pl.ds(0, cols)]
        block[...] = value.astype(bf16)
        copy = pltpu.make_async_copy(block, target, sems.at[slot])
        copy.start()
        copies.append(copy)

    def drain():
        for copy in copies[-n_slots:]:
            copy.wait()

    return send, drain


def grad_wdec(send, feat_ref, errs, wdec_ref, gbdec_ref, base, span, step):
    near = errs[0].shape[0]
    ones = jnp.ones((8, near), bf16)
    for low in range(0, span, step):
        cols = slice(low, min(low + step, span))
        value = sum(
            dot(feat_ref[:, side * near : (side + 1) * near], err[:, cols], 1, 0)
            for side, err in enumerate(errs)
        )
        send(value, wdec_ref.at[:, pl.ds(base + low, cols.stop - low)])
        gbdec_ref[:, cols] = sum(dot(ones, err[:, cols], 1, 0)[:1] for err in errs)


def early_body(
    step, feat_ref, w_dec_ref, near_ref, far_ref, wdec_ref, gbdec_ref, *rest
):
    near_out, far_out, buffer, sems = rest
    span = near_ref.shape[1]
    send, drain = sender(buffer, sems)
    grad_wdec(
        send, feat_ref, (near_ref, far_ref), wdec_ref, gbdec_ref, 0, span, step
    )
    weight = w_dec_ref[:, :span]
    near_out[...] = dot(near_ref[...], weight, 1, 1)
    far_out[...] = dot(far_ref[...], weight, 1, 1)
    drain()


def finish_body(
    step, entries, _, thr_ref, w_dec_ref, feat_ref, first_ref, second_ref, *rest
):
    pre_refs, partial_refs, err_refs = rest[:2], rest[2:4], rest[4:6]
    wenc_ref, wdec_ref, gthr_ref, gbenc_ref, gbdec_ref, loss_ref, buffer, sems = rest[6:]
    span = first_ref.shape[0]
    send, drain = sender(buffer, sems)
    weight = w_dec_ref[:, span:]
    grads, sums_thr, sums_benc = [], 0.0, 0.0
    for pre_ref, partial_ref, err_ref in zip(pre_refs, partial_refs, err_refs):
        grad_feat = partial_ref[...] + dot(err_ref[:, :span], weight, 1, 1)
        pre = pre_ref[...]
        soft = jax.nn.sigmoid((pre - thr_ref[...]) / gate_band)
        slope = soft * (1.0 - soft) / gate_band
        side_term = (grad_feat * pre + sparsity_coef) * slope
        grad = grad_feat * soft + side_term
        sums_thr = sums_thr - jnp.sum(side_term, axis=0, keepdims=True)
        sums_benc = sums_benc + jnp.sum(grad, axis=0, keepdims=True)
        grads.append(grad.astype(bf16))
    shares = sum(
        jnp.sum(err_ref[:, span:].astype(f32), axis=0, keepdims=True)
        for err_ref in err_refs
    )
    loss_ref[0, 0] = jnp.sum(shares) / entries
    gthr_ref[...] = sums_thr
    gbenc_ref[...] = sums_benc
    grads = jnp.concatenate(grads, axis=0)
    for i, layer_ref in enumerate((first_ref, second_ref)):
        for low in range(0, span, step):
            size = min(step, span - low)
            value = dot(layer_ref[low : low + size, :], grads, 1, 0)
            send(value, wenc_ref.at[pl.ds(i * span + low, size), :])
    grad_wdec(send, feat_ref, err_refs, wdec_ref, gbdec_ref, span, span, step)
    drain()


def program(n_dp, n_mp):
    n_z = n_mp // 2
    everyone = [(d, m) for d in range(n_dp) for m in range(n_mp)]

    bits_of = lambda count: [1 << i for i in range((count - 1).bit_length())]
    z_steps = [(0, bit) for bit in bits_of(n_z)]
    dp_steps = [(bit, 0) for bit in bits_of(n_dp)]
    orders = (z_steps + dp_steps, z_steps[::-1] + dp_steps[::-1])
    steps = len(orders[0])

    def other_core(value):
        return lax.ppermute(
            value, both, [(d * n_mp + m, d * n_mp + (m ^ 1)) for d, m in everyone]
        )

    def exchange(value, step):
        pairs = []
        for d, m in everyone:
            dp_bits, z_bits = orders[m % 2][step]
            pairs.append((d * n_mp + m, (d ^ dp_bits) * n_mp + (m ^ (2 * z_bits))))
        return lax.ppermute(value, both, pairs)

    def gather(rows):
        for step in range(steps):
            got = exchange(rows, step)
            rows = jnp.concatenate([rows, got], axis=0)
        return rows

    def scatter(total, count):
        for step in reversed(range(count)):
            cut = total.shape[0] // 2
            give = total[cut:].astype(bf16)
            got = exchange(give, step)
            total = total[:cut] + got.astype(f32)
        return total

    def whole_step(
        residual_in, pre_gain, post_gain, w_gate, w_up, w_down, w_enc, b_enc, threshold, w_dec, b_dec
    ):
        tokens, width = residual_in.shape[0] * n_dp, w_gate.shape[0]
        at_mp = lax.axis_index("mp")
        at_z, at_core = at_mp // 2, at_mp % 2
        count = residual_in.shape[0] // n_mp

        def columns(cuts):
            span = width // cuts
            return [slice(i * span, (i + 1) * span) for i in range(cuts)]

        full_rows = lax.all_gather(residual_in, "mp", axis=1, tiled=True)
        slot = jnp.arange(n_z)
        turned = sum(
            ((slot >> i) & 1) << (len(z_steps) - 1 - i) for i in range(len(z_steps))
        )
        straight = jnp.where(at_core == 0, slot, turned)
        crossed = jnp.where(at_core == 0, turned, slot)
        owner = jnp.concatenate(
            [2 * (at_z ^ straight) + at_core, 2 * (at_z ^ crossed) + 1 - at_core]
        )
        source = (owner[:, None] * count + jnp.arange(count)[None, :]).reshape(-1)
        pick = (source[:, None] == jnp.arange(source.shape[0])[None, :]).astype(bf16)
        full_rows = dot(pick, full_rows, 1, 0).astype(bf16)

        resid_wide = full_rows.astype(f32)
        normed = (
            resid_wide
            * lax.rsqrt(jnp.mean(resid_wide * resid_wide, axis=1, keepdims=True) + norm_eps)
            * pre_gain[None, :]
        ).astype(bf16)
        gate_out = dot(normed, w_gate, 1, 0)
        up_out = dot(normed, w_up, 1, 0)
        hidden = (jax.nn.gelu(gate_out, approximate=True) * up_out).astype(bf16)
        hidden = lax.optimization_barrier(hidden)
        half = hidden.shape[0] // 2
        blocks = []
        for cols in columns(2):
            part = dot(hidden, w_down[:, cols], 1, 0)
            mine = part[:half] + other_core(part[half:].astype(bf16)).astype(f32)
            blocks.append(scatter(mine, len(z_steps)))
        block = jnp.concatenate(blocks, axis=1)
        layer_own = (
            resid_wide[:count]
            + block
            * lax.rsqrt(jnp.mean(block * block, axis=1, keepdims=True) + norm_eps)
            * post_gain[None, :]
        ).astype(bf16)

        layer_out = []
        for cols in columns(2):
            near = gather(layer_own[:, cols])
            layer_out.append((near, other_core(near)))
        sides = range(2)

        cols = columns(2)
        pre_act = []
        for side in sides:
            first = dot(layer_out[0][side], w_enc[cols[0], :], 1, 0) + b_enc[None, :]
            first = lax.optimization_barrier(first)
            pre_act.append(first + dot(layer_out[1][side], w_enc[cols[1], :], 1, 0))
        soft = [jax.nn.sigmoid((pre - threshold[None, :]) / gate_band) for pre in pre_act]
        feat = [(pre * open_).astype(bf16) for pre, open_ in zip(pre_act, soft)]
        lanes = 128

        def fold(row):
            return sum(row[:, i : i + lanes] for i in range(0, row.shape[1], lanes))

        open_total = sum(
            fold(jnp.sum(open_, axis=0, keepdims=True)) for open_ in soft
        )
        error_own = []
        for cols in columns(2):
            far = other_core(dot(feat[1], w_dec[:, cols], 1, 0).astype(bf16))
            mine = dot(feat[0], w_dec[:, cols], 1, 0) + far.astype(f32)
            recon = scatter(mine, steps)
            error_own.append(recon + b_dec[None, cols] - layer_own[:, cols].astype(f32))

        rest = 0.5 * sum(
            fold(jnp.sum(error * error, axis=0, keepdims=True)) for error in error_own
        ) + sparsity_coef * open_total
        row = jnp.arange(count)[:, None]
        extra = jnp.zeros((count, lanes), f32)
        for i in range(3):
            term = lax.reduce_precision(rest, 8, 7)
            extra = jnp.where(row == i, term, extra)
            rest = rest - term
        extra = extra.astype(bf16)

        err_all = []
        for i, error in enumerate(error_own):
            rows = error.astype(bf16)
            if i == len(error_own) - 1:
                rows = jnp.concatenate([rows, extra], axis=1)
            near = gather(rows)
            err_all.append((near, other_core(near)))

        vmem = pl.BlockSpec(memory_space=pltpu.VMEM)
        hbm = pl.BlockSpec(memory_space=pl.ANY)
        features, span, step = w_enc.shape[1], width // 2, 512
        turned = []
        for pair in layer_out:
            turned.append(side_by_side(pair))
        threshold_row = row_of(threshold)
        feat_turned = side_by_side(feat)
        scratch = [
            pltpu.VMEM((4, max(step, features), max(step, features)), bf16),
            pltpu.SemaphoreType.DMA((4,)),
        ]
        params = pltpu.CompilerParams(vmem_limit_bytes=40 * 2**20)
        rows = pre_act[0].shape[0]
        grad_wdec, bdec_first, *partial = pl.pallas_call(
            functools.partial(early_body, step),
            out_shape=(
                jax.ShapeDtypeStruct((features, width), bf16),
                jax.ShapeDtypeStruct((1, span), f32),
                jax.ShapeDtypeStruct((rows, features), f32),
                jax.ShapeDtypeStruct((rows, features), f32),
            ),
            in_specs=[vmem] * 4,
            out_specs=(hbm, vmem, vmem, vmem),
            scratch_shapes=scratch,
            compiler_params=params,
            name="early",
        )(feat_turned, w_dec, *err_all[0])
        grad_wenc, grad_wdec, grad_thresh, grad_benc, bdec_second, loss = pl.pallas_call(
            functools.partial(finish_body, step, float(tokens * width)),
            out_shape=(
                jax.ShapeDtypeStruct((width, features), bf16),
                jax.ShapeDtypeStruct((features, width), bf16),
                jax.ShapeDtypeStruct((1, features), f32),
                jax.ShapeDtypeStruct((1, features), f32),
                jax.ShapeDtypeStruct((1, span), f32),
                jax.ShapeDtypeStruct((1, 1), f32),
            ),
            in_specs=[hbm] + [vmem] * 11,
            out_specs=(hbm, hbm, vmem, vmem, vmem, pl.BlockSpec(memory_space=pltpu.SMEM)),
            input_output_aliases={0: 1},
            scratch_shapes=scratch,
            compiler_params=params,
            name="finish",
        )(
            grad_wdec,
            threshold_row,
            w_dec,
            feat_turned,
            *turned,
            *pre_act,
            *partial,
            *err_all[1],
        )
        grad_bdec = jnp.concatenate([bdec_first, bdec_second], axis=1)[0]
        grad_thresh, grad_benc, loss_value = grad_thresh[0], grad_benc[0], loss[0, 0]
        return (loss_value, grad_wenc, grad_wdec, grad_benc, grad_thresh, grad_bdec)

    return whole_step


def solution(mesh):
    placed = (
        P("dp", "mp"),
        P(),
        P(),
        P(None, "mp"),
        P(None, "mp"),
        P("mp", None),
        P(None, both),
        P(both),
        P(both),
        P(both, None),
        P(),
    )
    return jax.shard_map(
        program(mesh.shape["dp"], mesh.shape["mp"]),
        mesh=mesh,
        in_specs=placed,
        out_specs=(P(), P(None, both), P(both, None), P(both), P(both), P()),
        check_vma=False,
    )
```

```python
import functools

import jax
import jax.numpy as jnp
from jax import lax
from jax.experimental import pallas as pl
from jax.experimental.pallas import tpu as pltpu
from jax.sharding import PartitionSpec as P


norm_eps = 1e-06
gate_band = 0.1
sparsity_coef = 0.05


f32 = jnp.float32
bf16 = jnp.bfloat16
both = ("dp", "mp")


def dot(left, right, left_dim, right_dim):
    return lax.dot_general(
        left, right, (((left_dim,), (right_dim,)), ((), ())), preferred_element_type=f32
    )


def turn_body(near_ref, far_ref, turned_ref):
    count = near_ref.shape[0]
    turned_ref[:, :count] = near_ref[...].T
    turned_ref[:, count:] = far_ref[...].T


def row_body(source_ref, row_ref):
    row_ref[...] = source_ref[...]


def row_of(values):
    vmem = pl.BlockSpec(memory_space=pltpu.VMEM)
    return pl.pallas_call(
        row_body,
        out_shape=jax.ShapeDtypeStruct((1, values.shape[0]), values.dtype),
        in_specs=[vmem],
        out_specs=vmem,
        name="row",
    )(values[None, :])


def side_by_side(pair):
    near, far = pair
    vmem = pl.BlockSpec(memory_space=pltpu.VMEM)
    return pl.pallas_call(
        turn_body,
        out_shape=jax.ShapeDtypeStruct((near.shape[1], 2 * near.shape[0]), near.dtype),
        in_specs=[vmem] * 2,
        out_specs=vmem,
        compiler_params=pltpu.CompilerParams(vmem_limit_bytes=40 * 2**20),
        name="turn",
    )(near, far)


def sender(buffer, sems):
    n_slots = buffer.shape[0]
    copies = []

    def send(value, target):
        index = len(copies)
        slot = index % n_slots
        if index >= n_slots:
            copies[index - n_slots].wait()
        rows, cols = value.shape
        block = buffer.at[slot, pl.ds(0, rows), pl.ds(0, cols)]
        block[...] = value.astype(bf16)
        copy = pltpu.make_async_copy(block, target, sems.at[slot])
        copy.start()
        copies.append(copy)

    def drain():
        for copy in copies[-n_slots:]:
            copy.wait()

    return send, drain


def grad_wdec(send, feat_ref, errs, wdec_ref, gbdec_ref, base, span, step):
    tokens = errs[0].shape[0]
    ones = jnp.ones((8, tokens), bf16)
    for low in range(0, span, step):
        cols = slice(low, min(low + step, span))
        value = sum(
            dot(feat_ref[:, i * tokens : (i + 1) * tokens], err[:, cols], 1, 0)
            for i, err in enumerate(errs)
        )
        send(value, wdec_ref.at[:, pl.ds(base + low, cols.stop - low)])
        gbdec_ref[:, cols] = sum(dot(ones, err[:, cols], 1, 0)[:1] for err in errs)


def early_body(
    step, feat_ref, w_dec_ref, near_ref, far_ref, wdec_ref, gbdec_ref, *rest
):
    near_out, far_out, buffer, sems = rest
    span = near_ref.shape[1]
    send, drain = sender(buffer, sems)
    grad_wdec(
        send, feat_ref, (near_ref, far_ref), wdec_ref, gbdec_ref, 0, span, step
    )
    weight = w_dec_ref[:, :span]
    near_out[...] = dot(near_ref[...], weight, 1, 1)
    far_out[...] = dot(far_ref[...], weight, 1, 1)
    drain()


def finish_body(
    step, entries, _, thr_ref, w_dec_ref, feat_ref, first_ref, second_ref, *rest
):
    pre_refs, partial_refs, err_refs = rest[:2], rest[2:4], rest[4:8]
    wenc_ref, wdec_ref, gthr_ref, gbenc_ref, gbdec_ref, loss_ref = rest[8:14]
    buffer, sems, whole_ref = rest[14:]
    span = first_ref.shape[0]
    piece = err_refs[0].shape[0]
    for i, err_ref in enumerate(err_refs):
        whole_ref[i * piece : (i + 1) * piece, :] = err_ref[:, :span]
    send, drain = sender(buffer, sems)
    weight = w_dec_ref[:, span:]
    grads, sums_thr, sums_benc = [], 0.0, 0.0
    for side, (pre_ref, partial_ref) in enumerate(zip(pre_refs, partial_refs)):
        rows = slice(2 * side * piece, 2 * (side + 1) * piece)
        grad_feat = partial_ref[...] + dot(whole_ref[rows, :], weight, 1, 1)
        pre = pre_ref[...]
        soft = jax.nn.sigmoid((pre - thr_ref[...]) / gate_band)
        slope = soft * (1.0 - soft) / gate_band
        side_term = (grad_feat * pre + sparsity_coef) * slope
        grad = grad_feat * soft + side_term
        sums_thr = sums_thr - jnp.sum(side_term, axis=0, keepdims=True)
        sums_benc = sums_benc + jnp.sum(grad, axis=0, keepdims=True)
        grads.append(grad.astype(bf16))
    shares = sum(
        jnp.sum(err_ref[:, span:].astype(f32), axis=0, keepdims=True)
        for err_ref in err_refs
    )
    loss_ref[0, 0] = jnp.sum(shares) / entries
    gthr_ref[...] = sums_thr
    gbenc_ref[...] = sums_benc
    grads = jnp.concatenate(grads, axis=0)
    for i, layer_ref in enumerate((first_ref, second_ref)):
        for low in range(0, span, step):
            size = min(step, span - low)
            value = dot(layer_ref[low : low + size, :], grads, 1, 0)
            send(value, wenc_ref.at[pl.ds(i * span + low, size), :])
    grad_wdec(send, feat_ref, (whole_ref,), wdec_ref, gbdec_ref, span, span, step)
    drain()


def program(n_dp, n_mp):
    n_z = n_mp // 2
    everyone = [(d, m) for d in range(n_dp) for m in range(n_mp)]

    bits_of = lambda count: [1 << i for i in range((count - 1).bit_length())]
    z_steps = [(0, bit) for bit in bits_of(n_z)]
    dp_steps = [(bit, 0) for bit in bits_of(n_dp)]
    orders = (z_steps + dp_steps, z_steps[::-1] + dp_steps[::-1])
    steps = len(orders[0])

    def other_core(value):
        return lax.ppermute(
            value, both, [(d * n_mp + m, d * n_mp + (m ^ 1)) for d, m in everyone]
        )

    def exchange(value, step):
        pairs = []
        for d, m in everyone:
            dp_bits, z_bits = orders[m % 2][step]
            pairs.append((d * n_mp + m, (d ^ dp_bits) * n_mp + (m ^ (2 * z_bits))))
        return lax.ppermute(value, both, pairs)

    def gather(rows, apart=False):
        for step in range(steps):
            got = exchange(rows, step)
            if apart and step == steps - 1:
                return rows, got
            rows = jnp.concatenate([rows, got], axis=0)
        return rows

    def scatter(total, count):
        for step in reversed(range(count)):
            cut = total.shape[0] // 2
            give = total[cut:].astype(bf16)
            got = exchange(give, step)
            total = total[:cut] + got.astype(f32)
        return total

    def whole_step(
        residual_in, pre_gain, post_gain, w_gate, w_up, w_down, w_enc, b_enc, threshold, w_dec, b_dec
    ):
        tokens, width = residual_in.shape[0] * n_dp, w_gate.shape[0]
        at_mp = lax.axis_index("mp")
        at_z, at_core = at_mp // 2, at_mp % 2
        count = residual_in.shape[0] // n_mp

        def columns(cuts):
            span = width // cuts
            return [slice(i * span, (i + 1) * span) for i in range(cuts)]

        full_rows = lax.all_gather(residual_in, "mp", axis=1, tiled=True)
        slot = jnp.arange(n_z)
        turned = sum(
            ((slot >> i) & 1) << (len(z_steps) - 1 - i) for i in range(len(z_steps))
        )
        straight = jnp.where(at_core == 0, slot, turned)
        crossed = jnp.where(at_core == 0, turned, slot)
        owner = jnp.concatenate(
            [2 * (at_z ^ straight) + at_core, 2 * (at_z ^ crossed) + 1 - at_core]
        )
        source = (owner[:, None] * count + jnp.arange(count)[None, :]).reshape(-1)
        pick = (source[:, None] == jnp.arange(source.shape[0])[None, :]).astype(bf16)
        full_rows = dot(pick, full_rows, 1, 0).astype(bf16)

        resid_wide = full_rows.astype(f32)
        normed = (
            resid_wide
            * lax.rsqrt(jnp.mean(resid_wide * resid_wide, axis=1, keepdims=True) + norm_eps)
            * pre_gain[None, :]
        ).astype(bf16)
        gate_out = dot(normed, w_gate, 1, 0)
        up_out = dot(normed, w_up, 1, 0)
        hidden = (jax.nn.gelu(gate_out, approximate=True) * up_out).astype(bf16)
        hidden = lax.optimization_barrier(hidden)
        half = hidden.shape[0] // 2
        blocks = []
        for cols in columns(2):
            part = dot(hidden, w_down[:, cols], 1, 0)
            mine = part[:half] + other_core(part[half:].astype(bf16)).astype(f32)
            blocks.append(scatter(mine, len(z_steps)))
        block = jnp.concatenate(blocks, axis=1)
        layer_own = (
            resid_wide[:count]
            + block
            * lax.rsqrt(jnp.mean(block * block, axis=1, keepdims=True) + norm_eps)
            * post_gain[None, :]
        ).astype(bf16)

        layer_out = []
        for cols in columns(2):
            near = gather(layer_own[:, cols])
            layer_out.append((near, other_core(near)))
        sides = range(2)

        cols = columns(2)
        pre_act = []
        for side in sides:
            first = dot(layer_out[0][side], w_enc[cols[0], :], 1, 0) + b_enc[None, :]
            first = lax.optimization_barrier(first)
            pre_act.append(first + dot(layer_out[1][side], w_enc[cols[1], :], 1, 0))
        soft = [jax.nn.sigmoid((pre - threshold[None, :]) / gate_band) for pre in pre_act]
        feat = [(pre * open_).astype(bf16) for pre, open_ in zip(pre_act, soft)]
        lanes = 128

        def fold(row):
            return sum(row[:, i : i + lanes] for i in range(0, row.shape[1], lanes))

        open_total = sum(
            fold(jnp.sum(open_, axis=0, keepdims=True)) for open_ in soft
        )
        error_own = []
        for cols in columns(2):
            far = other_core(dot(feat[1], w_dec[:, cols], 1, 0).astype(bf16))
            mine = dot(feat[0], w_dec[:, cols], 1, 0) + far.astype(f32)
            recon = scatter(mine, steps)
            error_own.append(recon + b_dec[None, cols] - layer_own[:, cols].astype(f32))

        rest = 0.5 * sum(
            fold(jnp.sum(error * error, axis=0, keepdims=True)) for error in error_own
        ) + sparsity_coef * open_total
        row = jnp.arange(count)[:, None]
        extra = jnp.zeros((count, lanes), f32)
        for i in range(3):
            term = lax.reduce_precision(rest, 8, 7)
            extra = jnp.where(row == i, term, extra)
            rest = rest - term
        extra = extra.astype(bf16)

        err_all = []
        for i, error in enumerate(error_own):
            rows = error.astype(bf16)
            if i == len(error_own) - 1:
                rows = jnp.concatenate([rows, extra], axis=1)
            if i == len(error_own) - 1:
                pieces = gather(rows, apart=True)
                err_last = (*pieces, *(other_core(piece) for piece in pieces))
            else:
                near = gather(rows)
                err_all.append((near, other_core(near)))

        vmem = pl.BlockSpec(memory_space=pltpu.VMEM)
        hbm = pl.BlockSpec(memory_space=pl.ANY)
        features, span, step = w_enc.shape[1], width // 2, 512
        turned = []
        for pair in layer_out:
            turned.append(side_by_side(pair))
        threshold_row = row_of(threshold)
        feat_turned = side_by_side(feat)
        scratch = [
            pltpu.VMEM((4, max(step, features), max(step, features)), bf16),
            pltpu.SemaphoreType.DMA((4,)),
        ]
        params = pltpu.CompilerParams(vmem_limit_bytes=40 * 2**20)
        rows = pre_act[0].shape[0]
        grad_wdec, bdec_first, *partial = pl.pallas_call(
            functools.partial(early_body, step),
            out_shape=(
                jax.ShapeDtypeStruct((features, width), bf16),
                jax.ShapeDtypeStruct((1, span), f32),
                jax.ShapeDtypeStruct((rows, features), f32),
                jax.ShapeDtypeStruct((rows, features), f32),
            ),
            in_specs=[vmem] * 4,
            out_specs=(hbm, vmem, vmem, vmem),
            scratch_shapes=scratch,
            compiler_params=params,
            name="early",
        )(feat_turned, w_dec, *err_all[0])
        grad_wenc, grad_wdec, grad_thresh, grad_benc, bdec_second, loss = pl.pallas_call(
            functools.partial(finish_body, step, float(tokens * width)),
            out_shape=(
                jax.ShapeDtypeStruct((width, features), bf16),
                jax.ShapeDtypeStruct((features, width), bf16),
                jax.ShapeDtypeStruct((1, features), f32),
                jax.ShapeDtypeStruct((1, features), f32),
                jax.ShapeDtypeStruct((1, span), f32),
                jax.ShapeDtypeStruct((1, 1), f32),
            ),
            in_specs=[hbm] + [vmem] * 13,
            out_specs=(hbm, hbm, vmem, vmem, vmem, pl.BlockSpec(memory_space=pltpu.SMEM)),
            input_output_aliases={0: 1},
            scratch_shapes=scratch + [pltpu.VMEM((2 * rows, span), bf16)],
            compiler_params=params,
            name="finish",
        )(
            grad_wdec,
            threshold_row,
            w_dec,
            feat_turned,
            *turned,
            *pre_act,
            *partial,
            *err_last,
        )
        grad_bdec = jnp.concatenate([bdec_first, bdec_second], axis=1)[0]
        grad_thresh, grad_benc, loss_value = grad_thresh[0], grad_benc[0], loss[0, 0]
        return (loss_value, grad_wenc, grad_wdec, grad_benc, grad_thresh, grad_bdec)

    return whole_step


def solution(mesh):
    placed = (
        P("dp", "mp"),
        P(),
        P(),
        P(None, "mp"),
        P(None, "mp"),
        P("mp", None),
        P(None, both),
        P(both),
        P(both),
        P(both, None),
        P(),
    )
    return jax.shard_map(
        program(mesh.shape["dp"], mesh.shape["mp"]),
        mesh=mesh,
        in_specs=placed,
        out_specs=(P(), P(None, both), P(both, None), P(both), P(both), P()),
        check_vma=False,
    )
```

```python
import functools

import jax
import jax.numpy as jnp
from jax import lax
from jax.experimental import pallas as pl
from jax.experimental.pallas import tpu as pltpu
from jax.sharding import PartitionSpec as P


norm_eps = 1e-06
gate_band = 0.1
sparsity_coef = 0.05


f32 = jnp.float32
bf16 = jnp.bfloat16
both = ("dp", "mp")


def dot(left, right, left_dim, right_dim):
    return lax.dot_general(
        left, right, (((left_dim,), (right_dim,)), ((), ())), preferred_element_type=f32
    )


def turn_body(near_ref, far_ref, turned_ref):
    count = near_ref.shape[0]
    turned_ref[:, :count] = near_ref[...].T
    turned_ref[:, count:] = far_ref[...].T


def row_body(source_ref, _, row_ref):
    row_ref[...] = source_ref[...]


def row_of(values, weight):
    vmem = pl.BlockSpec(memory_space=pltpu.VMEM)
    return pl.pallas_call(
        row_body,
        out_shape=jax.ShapeDtypeStruct((1, values.shape[0]), values.dtype),
        in_specs=[vmem, pl.BlockSpec(memory_space=pl.ANY)],
        out_specs=vmem,
        name="row",
    )(values[None, :], weight)


def side_by_side(pair):
    near, far = pair
    vmem = pl.BlockSpec(memory_space=pltpu.VMEM)
    return pl.pallas_call(
        turn_body,
        out_shape=jax.ShapeDtypeStruct((near.shape[1], 2 * near.shape[0]), near.dtype),
        in_specs=[vmem] * 2,
        out_specs=vmem,
        compiler_params=pltpu.CompilerParams(vmem_limit_bytes=40 * 2**20),
        name="turn",
    )(near, far)


def sender(buffer, sems):
    n_slots = buffer.shape[0]
    copies = []

    def send(value, target):
        index = len(copies)
        slot = index % n_slots
        if index >= n_slots:
            copies[index - n_slots].wait()
        rows, cols = value.shape
        block = buffer.at[slot, pl.ds(0, rows), pl.ds(0, cols)]
        block[...] = value.astype(bf16)
        copy = pltpu.make_async_copy(block, target, sems.at[slot])
        copy.start()
        copies.append(copy)

    def drain():
        for copy in copies[-n_slots:]:
            copy.wait()

    return send, drain


def grad_wdec(send, feat_ref, errs, wdec_ref, gbdec_ref, base, span, step):
    tokens = errs[0].shape[0]
    ones = jnp.ones((8, tokens), bf16)
    for low in range(0, span, step):
        cols = slice(low, min(low + step, span))
        value = sum(
            dot(feat_ref[:, i * tokens : (i + 1) * tokens], err[:, cols], 1, 0)
            for i, err in enumerate(errs)
        )
        send(value, wdec_ref.at[:, pl.ds(base + low, cols.stop - low)])
        gbdec_ref[:, cols] = sum(dot(ones, err[:, cols], 1, 0)[:1] for err in errs)


def early_body(
    step, feat_ref, w_dec_ref, near_ref, far_ref, wdec_ref, gbdec_ref, *rest
):
    near_out, far_out, buffer, sems = rest
    span = near_ref.shape[1]
    send, drain = sender(buffer, sems)
    grad_wdec(
        send, feat_ref, (near_ref, far_ref), wdec_ref, gbdec_ref, 0, span, step
    )
    weight = w_dec_ref[:, :span]
    near_out[...] = dot(near_ref[...], weight, 1, 1)
    far_out[...] = dot(far_ref[...], weight, 1, 1)
    drain()


def finish_body(
    step, entries, _, thr_ref, w_dec_ref, feat_ref, first_ref, second_ref, *rest
):
    pre_refs, partial_refs, err_refs = rest[:2], rest[2:4], rest[4:8]
    wenc_ref, wdec_ref, gthr_ref, gbenc_ref, gbdec_ref, loss_ref = rest[8:14]
    buffer, sems, whole_ref = rest[14:]
    span = first_ref.shape[0]
    piece = err_refs[0].shape[0]
    for i, err_ref in enumerate(err_refs):
        whole_ref[i * piece : (i + 1) * piece, :] = err_ref[:, :span]
    send, drain = sender(buffer, sems)
    weight = w_dec_ref[:, span:]
    grads, sums_thr, sums_benc = [], 0.0, 0.0
    for side, (pre_ref, partial_ref) in enumerate(zip(pre_refs, partial_refs)):
        rows = slice(2 * side * piece, 2 * (side + 1) * piece)
        grad_feat = partial_ref[...] + dot(whole_ref[rows, :], weight, 1, 1)
        pre = pre_ref[...]
        soft = jax.nn.sigmoid((pre - thr_ref[...]) / gate_band)
        slope = soft * (1.0 - soft) / gate_band
        side_term = (grad_feat * pre + sparsity_coef) * slope
        grad = grad_feat * soft + side_term
        sums_thr = sums_thr - jnp.sum(side_term, axis=0, keepdims=True)
        sums_benc = sums_benc + jnp.sum(grad, axis=0, keepdims=True)
        grads.append(grad.astype(bf16))
    shares = sum(
        jnp.sum(err_ref[:, span:].astype(f32), axis=0, keepdims=True)
        for err_ref in err_refs
    )
    loss_ref[0, 0] = jnp.sum(shares) / entries
    gthr_ref[...] = sums_thr
    gbenc_ref[...] = sums_benc
    grads = jnp.concatenate(grads, axis=0)
    for i, layer_ref in enumerate((first_ref, second_ref)):
        for low in range(0, span, step):
            size = min(step, span - low)
            value = dot(layer_ref[low : low + size, :], grads, 1, 0)
            send(value, wenc_ref.at[pl.ds(i * span + low, size), :])
    grad_wdec(send, feat_ref, (whole_ref,), wdec_ref, gbdec_ref, span, span, step)
    drain()


def program(n_dp, n_mp):
    n_z = n_mp // 2
    everyone = [(d, m) for d in range(n_dp) for m in range(n_mp)]

    bits_of = lambda count: [1 << i for i in range((count - 1).bit_length())]
    z_steps = [(0, bit) for bit in bits_of(n_z)]
    dp_steps = [(bit, 0) for bit in bits_of(n_dp)]
    orders = (z_steps + dp_steps, z_steps[::-1] + dp_steps[::-1])
    steps = len(orders[0])

    def other_core(value):
        return lax.ppermute(
            value, both, [(d * n_mp + m, d * n_mp + (m ^ 1)) for d, m in everyone]
        )

    def exchange(value, step):
        pairs = []
        for d, m in everyone:
            dp_bits, z_bits = orders[m % 2][step]
            pairs.append((d * n_mp + m, (d ^ dp_bits) * n_mp + (m ^ (2 * z_bits))))
        return lax.ppermute(value, both, pairs)

    def gather(rows, apart=False):
        for step in range(steps):
            got = exchange(rows, step)
            if apart and step == steps - 1:
                return rows, got
            rows = jnp.concatenate([rows, got], axis=0)
        return rows

    def scatter(total, count):
        for step in reversed(range(count)):
            cut = total.shape[0] // 2
            give = total[cut:].astype(bf16)
            got = exchange(give, step)
            total = total[:cut] + got.astype(f32)
        return total

    def whole_step(
        residual_in, pre_gain, post_gain, w_gate, w_up, w_down, w_enc, b_enc, threshold, w_dec, b_dec
    ):
        tokens, width = residual_in.shape[0] * n_dp, w_gate.shape[0]
        at_mp = lax.axis_index("mp")
        at_z, at_core = at_mp // 2, at_mp % 2
        count = residual_in.shape[0] // n_mp

        def columns(cuts):
            span = width // cuts
            return [slice(i * span, (i + 1) * span) for i in range(cuts)]

        full_rows = lax.all_gather(residual_in, "mp", axis=1, tiled=True)
        slot = jnp.arange(n_z)
        turned = sum(
            ((slot >> i) & 1) << (len(z_steps) - 1 - i) for i in range(len(z_steps))
        )
        straight = jnp.where(at_core == 0, slot, turned)
        crossed = jnp.where(at_core == 0, turned, slot)
        owner = jnp.concatenate(
            [2 * (at_z ^ straight) + at_core, 2 * (at_z ^ crossed) + 1 - at_core]
        )
        source = (owner[:, None] * count + jnp.arange(count)[None, :]).reshape(-1)
        pick = (source[:, None] == jnp.arange(source.shape[0])[None, :]).astype(bf16)
        full_rows = dot(pick, full_rows, 1, 0).astype(bf16)

        resid_wide = full_rows.astype(f32)
        normed = (
            resid_wide
            * lax.rsqrt(jnp.mean(resid_wide * resid_wide, axis=1, keepdims=True) + norm_eps)
            * pre_gain[None, :]
        ).astype(bf16)
        gate_out = dot(normed, w_gate, 1, 0)
        up_out = dot(normed, w_up, 1, 0)
        hidden = (jax.nn.gelu(gate_out, approximate=True) * up_out).astype(bf16)
        hidden = lax.optimization_barrier(hidden)
        half = hidden.shape[0] // 2
        blocks = []
        for cols in columns(2):
            part = dot(hidden, w_down[:, cols], 1, 0)
            mine = part[:half] + other_core(part[half:].astype(bf16)).astype(f32)
            blocks.append(scatter(mine, len(z_steps)))
        block = jnp.concatenate(blocks, axis=1)
        layer_own = (
            resid_wide[:count]
            + block
            * lax.rsqrt(jnp.mean(block * block, axis=1, keepdims=True) + norm_eps)
            * post_gain[None, :]
        ).astype(bf16)

        layer_out = []
        for cols in columns(2):
            near = gather(layer_own[:, cols])
            layer_out.append((near, other_core(near)))
        sides = range(2)

        cols = columns(2)
        pre_act = []
        for side in sides:
            first = dot(layer_out[0][side], w_enc[cols[0], :], 1, 0) + b_enc[None, :]
            first = lax.optimization_barrier(first)
            pre_act.append(first + dot(layer_out[1][side], w_enc[cols[1], :], 1, 0))
        soft = [jax.nn.sigmoid((pre - threshold[None, :]) / gate_band) for pre in pre_act]
        feat = [(pre * open_).astype(bf16) for pre, open_ in zip(pre_act, soft)]
        lanes = 128

        def fold(row):
            return sum(row[:, i : i + lanes] for i in range(0, row.shape[1], lanes))

        open_total = sum(
            fold(jnp.sum(open_, axis=0, keepdims=True)) for open_ in soft
        )
        error_own = []
        for cols in columns(2):
            far = other_core(dot(feat[1], w_dec[:, cols], 1, 0).astype(bf16))
            mine = dot(feat[0], w_dec[:, cols], 1, 0) + far.astype(f32)
            recon = scatter(mine, steps)
            error_own.append(recon + b_dec[None, cols] - layer_own[:, cols].astype(f32))

        rest = 0.5 * sum(
            fold(jnp.sum(error * error, axis=0, keepdims=True)) for error in error_own
        ) + sparsity_coef * open_total
        row = jnp.arange(count)[:, None]
        extra = jnp.zeros((count, lanes), f32)
        for i in range(3):
            term = lax.reduce_precision(rest, 8, 7)
            extra = jnp.where(row == i, term, extra)
            rest = rest - term
        extra = extra.astype(bf16)

        err_all = []
        for i, error in enumerate(error_own):
            rows = error.astype(bf16)
            if i == len(error_own) - 1:
                rows = jnp.concatenate([rows, extra], axis=1)
            if i == len(error_own) - 1:
                pieces = gather(rows, apart=True)
                err_last = (*pieces, *(other_core(piece) for piece in pieces))
            else:
                near = gather(rows)
                err_all.append((near, other_core(near)))

        vmem = pl.BlockSpec(memory_space=pltpu.VMEM)
        hbm = pl.BlockSpec(memory_space=pl.ANY)
        features, span, step = w_enc.shape[1], width // 2, 512
        turned = []
        for pair in layer_out:
            turned.append(side_by_side(pair))
        threshold_row = row_of(threshold, w_dec)
        feat_turned = side_by_side(feat)
        scratch = [
            pltpu.VMEM((4, max(step, features), max(step, features)), bf16),
            pltpu.SemaphoreType.DMA((4,)),
        ]
        params = pltpu.CompilerParams(vmem_limit_bytes=40 * 2**20)
        rows = pre_act[0].shape[0]
        grad_wdec, bdec_first, *partial = pl.pallas_call(
            functools.partial(early_body, step),
            out_shape=(
                jax.ShapeDtypeStruct((features, width), bf16),
                jax.ShapeDtypeStruct((1, span), f32),
                jax.ShapeDtypeStruct((rows, features), f32),
                jax.ShapeDtypeStruct((rows, features), f32),
            ),
            in_specs=[vmem] * 4,
            out_specs=(hbm, vmem, vmem, vmem),
            scratch_shapes=scratch,
            compiler_params=params,
            name="early",
        )(feat_turned, w_dec, *err_all[0])
        grad_wenc, grad_wdec, grad_thresh, grad_benc, bdec_second, loss = pl.pallas_call(
            functools.partial(finish_body, step, float(tokens * width)),
            out_shape=(
                jax.ShapeDtypeStruct((width, features), bf16),
                jax.ShapeDtypeStruct((features, width), bf16),
                jax.ShapeDtypeStruct((1, features), f32),
                jax.ShapeDtypeStruct((1, features), f32),
                jax.ShapeDtypeStruct((1, span), f32),
                jax.ShapeDtypeStruct((1, 1), f32),
            ),
            in_specs=[hbm] + [vmem] * 13,
            out_specs=(hbm, hbm, vmem, vmem, vmem, pl.BlockSpec(memory_space=pltpu.SMEM)),
            input_output_aliases={0: 1},
            scratch_shapes=scratch + [pltpu.VMEM((2 * rows, span), bf16)],
            compiler_params=params,
            name="finish",
        )(
            grad_wdec,
            threshold_row,
            w_dec,
            feat_turned,
            *turned,
            *pre_act,
            *partial,
            *err_last,
        )
        grad_bdec = jnp.concatenate([bdec_first, bdec_second], axis=1)[0]
        grad_thresh, grad_benc, loss_value = grad_thresh[0], grad_benc[0], loss[0, 0]
        return (loss_value, grad_wenc, grad_wdec, grad_benc, grad_thresh, grad_bdec)

    return whole_step


def solution(mesh):
    placed = (
        P("dp", "mp"),
        P(),
        P(),
        P(None, "mp"),
        P(None, "mp"),
        P("mp", None),
        P(None, both),
        P(both),
        P(both),
        P(both, None),
        P(),
    )
    return jax.shard_map(
        program(mesh.shape["dp"], mesh.shape["mp"]),
        mesh=mesh,
        in_specs=placed,
        out_specs=(P(), P(None, both), P(both, None), P(both), P(both), P()),
        check_vma=False,
    )
```
